32 devices in a mesh: sec: 2 (over core), blk: 16 (over z, y, x).
Axes of the slice: x: 2, y: 2, z: 4, core: 2. Of those that a mesh axis runs over, the one named last changes fastest.
Arguments:
- density: float32 [64, 32, 128], P('blk', 'sec'), may hold values from 0.5 to 2
- velocity: float32 [3, 64, 32, 128], P(None, 'blk', 'sec'), may hold values from -3 to 3
- magnetic: float32 [3, 64, 32, 128], P(None, 'blk', 'sec'), may hold values from -2.5 to 2.5
- pressure: float32 [64, 32, 128], P('blk', 'sec'), may hold values from 0.5 to 2
- shell_source: int32 [2, 32, 128], P(None, 'sec'), may hold values from 0 to 4095
Outputs:
- state: float32 [8, 64, 32, 128], P(None, 'blk', 'sec')
The draws below stay inside these ranges and needn't reach their ends.
Inputs may be any that keep to these rules, and one draw needn't show every extreme that they name: `shell_source`: each entry is a flat index y * 128 + z into one 32 x 128 layer.
All inputs are finite; a program needn't handle non-finite values.
Results may differ from the reference program's by a relative error of at most 0.0001.
Values sent between devices are 32-bit elements; how exact they have to be, the bound alone decides.
A program may use at most 64 MiB of HBM per device.

```python
import math
import jax
import jax.numpy as jnp
from jax import lax

LX = 4
LZ = 128
STEPS = 2
NX = 64
NY = 32
CORONA_BLK = 8
HELIO_BLK = 6


def with_ends(values, rng, smallest, high):
    longest = values.shape.index(max(values.shape))
    spots = []
    for shift in (0, 1):
        where = [jax.random.randint(jax.random.fold_in(rng, axis), (), 0, length) for axis, length in enumerate(values.shape)]
        where[longest] = (where[longest] + shift) % values.shape[longest]
        spots.append(tuple(where))
    return values.at[spots[0]].set(smallest).at[spots[1]].set(high)


def steps_of(key, extent, cuts, low, largest):
    def one(position, parts):
        steps = jax.random.uniform(jax.random.fold_in(jax.random.fold_in(key, 6), position), (parts,), jnp.float32, low / len(cuts), largest / len(cuts))
        return jnp.repeat(jnp.exp(steps), extent[position] // parts).reshape((-1,) + (1,) * (len(extent) - position - 1))

    level = one(*cuts[0])
    for cut in cuts[1:]:
        level = level * one(*cut)
    return level


def noise(key, shape, spread, most, shards=(), dtype=jnp.bfloat16):
    values = jax.random.normal(key, shape, jnp.float32) * spread
    if len(shards) > 0:
        values = steps_of(key, shape, shards, -0.22, 0.18) * values
    return jnp.clip(values, min=-most, max=most).astype(dtype)


def setup_inputs(seed: int = 0) -> dict:
    seeds = jax.random.split(jax.random.key(seed), 6)
    density = jnp.clip(jnp.exp(math.log(2.0) - 1.3862944 * jax.random.uniform(seeds[0], (NX, NY, LZ), jnp.float32) ** steps_of(seeds[0], (NX, NY, LZ), ((0, 16), (1, 2)), -0.2, 0.2)), 0.5, 2.0)
    velocity = noise(seeds[1], (3, NX, NY, LZ), 0.3, 3.0, ((1, 16), (2, 2)), jnp.float32)
    magnetic = noise(seeds[2], (3, NX, NY, LZ), 0.4, 2.5, ((1, 16), (2, 2)), jnp.float32)
    pressure = jnp.clip(jnp.exp(math.log(2.0) - 1.3862944 * jax.random.uniform(seeds[3], (NX, NY, LZ), jnp.float32) ** steps_of(seeds[3], (NX, NY, LZ), ((0, 16), (1, 2)), -0.2, 0.2)), 0.5, 2.0)
    shell_source = with_ends(jax.random.randint(seeds[4], (2, NY, LZ), 0, NY * LZ), jax.random.fold_in(seeds[4], 1), 0, (NY * LZ) - 1).astype(jnp.int32)
    return dict(density=density, velocity=velocity, magnetic=magnetic, pressure=pressure, shell_source=shell_source)


GAMMA = 5.0 / 3.0

def conserve(density, velocity, magnetic, pressure):
    kinetic = 0.5 * density * lax.optimization_barrier(jnp.sum(velocity * velocity, 0))
    field_energy = 0.5 * lax.optimization_barrier(jnp.sum(magnetic * magnetic, 0))
    energy = pressure / (GAMMA - 1.0) + kinetic + field_energy
    return jnp.concatenate([density[None], density[None] * velocity, magnetic, energy[None]], 0)

def physical(cells, direction):
    rho = cells[0]
    vel = cells[1:4] / rho
    mag = cells[4:7]
    energy = cells[7]
    bsq = lax.optimization_barrier(jnp.sum(mag * mag, 0))
    vsq = lax.optimization_barrier(jnp.sum(vel * vel, 0))
    vdotb = lax.optimization_barrier(jnp.sum(vel * mag, 0))
    pres = (GAMMA - 1.0) * (energy - 0.5 * rho * vsq - 0.5 * bsq)
    ptot = pres + 0.5 * bsq
    normal_v = vel[direction]
    normal_b = mag[direction]
    unit = (jnp.arange(3) == direction).astype(jnp.float32)[:, None, None, None]
    momentum = rho * vel * normal_v - mag * normal_b + ptot * unit
    induction = normal_v * mag - normal_b * vel
    power = (energy + ptot) * normal_v - normal_b * vdotb
    flux = jnp.concatenate([(rho * normal_v)[None], momentum, induction, power[None]], 0)
    speed = jnp.abs(normal_v) + jnp.sqrt((GAMMA * (GAMMA - 1.0) * energy + bsq) / rho)
    return (flux, speed)

def face_flux(left, right, direction):
    flux_left, speed_left = physical(left, direction)
    flux_right, speed_right = physical(right, direction)
    reach = jnp.maximum(speed_left, speed_right)
    return 0.5 * (flux_left + flux_right) - 0.5 * reach * (right - left)

def divergence(padded, axis, direction):
    size = padded.shape[axis]
    left = lax.slice_in_dim(padded, 0, size - 1, axis=axis)
    right = lax.slice_in_dim(padded, 1, size, axis=axis)
    faces = face_flux(left, right, direction)
    return lax.slice_in_dim(faces, 1, size - 1, axis=axis) - lax.slice_in_dim(faces, 0, size - 2, axis=axis)

def update(sub, inner, outer, coeff):
    xpad = jnp.concatenate([inner, sub, outer], 1)
    ypad = jnp.concatenate([sub[:, :, -1:], sub, sub[:, :, :1]], 2)
    zpad = jnp.concatenate([sub[..., :1], sub, sub[..., -1:]], 3)
    total = divergence(xpad, 1, 0) + divergence(ypad, 2, 1) + divergence(zpad, 3, 2)
    return sub - coeff * total

def advance(state, shell_source):
    first = CORONA_BLK * LX
    second = (CORONA_BLK + HELIO_BLK) * LX
    bounds = [(0, first, 0.05), (first, second, 0.04), (second, NX, 0.055)]
    pieces = []
    for which in range(3):
        start, stop, coeff = bounds[which]
        sub = state[:, start:stop]
        if which == 0:
            inner = sub[:, :1]
        else:
            face = state[:, start - 1].reshape(8, -1)
            inner = face[:, shell_source[which - 1].reshape(-1)].reshape(8, NY, LZ)[:, None]
        if which == 2:
            outer = sub[:, -1:]
        else:
            outer = state[:, stop:stop + 1]
        pieces.append(update(sub, inner, outer, coeff))
    return jnp.concatenate(pieces, 1)

def reference(density, velocity, magnetic, pressure, shell_source):
    state = conserve(density, velocity, magnetic, pressure)
    for step in range(STEPS):
        state = advance(state, shell_source)
    return state
```

```python
import functools
import jax
import jax.numpy as jnp
from jax import lax
from jax.experimental import pallas as pl
from jax.experimental.pallas import tpu as pltpu
from jax.sharding import PartitionSpec as P

GAMMA = 5.0 / 3.0
MESH = pl.DeviceIdType.MESH


def conserve(raw):
    rho, v, b, p = raw[0], raw[1:4], raw[4:7], raw[7]
    vsq = v[0] * v[0] + v[1] * v[1] + v[2] * v[2]
    bsq = b[0] * b[0] + b[1] * b[1] + b[2] * b[2]
    energy = p * (1.0 / (GAMMA - 1.0)) + 0.5 * rho * vsq + 0.5 * bsq
    return [rho, rho * v[0], rho * v[1], rho * v[2], b[0], b[1], b[2], energy]


def shared(u):
    inv = 1.0 / u[0]
    v = [u[1] * inv, u[2] * inv, u[3] * inv]
    b = u[4:7]
    bsq = b[0] * b[0] + b[1] * b[1] + b[2] * b[2]
    mv = u[1] * v[0] + u[2] * v[1] + u[3] * v[2]
    vb = v[0] * b[0] + v[1] * b[1] + v[2] * b[2]
    half = 0.5 * bsq
    ptot = (GAMMA - 1.0) * (u[7] - 0.5 * mv - half) + half
    fast = jnp.sqrt((GAMMA * (GAMMA - 1.0) * u[7] + bsq) * inv)
    return v, vb, ptot, u[7] + ptot, fast


def flux(u, sh, d):
    v, vb, ptot, ep, fast = sh
    vd, bd = v[d], u[4 + d]
    mom = [u[1 + i] * vd - u[4 + i] * bd for i in range(3)]
    mom[d] = mom[d] + ptot
    ind = [vd * u[4 + i] - bd * v[i] if i != d else None for i in range(3)]
    return [u[1 + d]] + mom + ind + [ep * vd - bd * vb], jnp.abs(vd) + fast


def face(ul, fl, sl, ur, fr, sr):
    reach = jnp.maximum(sl, sr)
    out = []
    for k in range(8):
        jump = reach * (ur[k] - ul[k])
        out.append(-jump if fl[k] is None else (fl[k] + fr[k]) - jump)
    return out


def along_z(u, sh):
    f, s = flux(u, sh, 2)
    lanes = u[0].shape[1]
    lane = lax.broadcasted_iota(jnp.int32, u[0].shape, 1)
    last, first = lane == lanes - 1, lane == 0
    nxt = lambda x: None if x is None else pltpu.roll(x, lanes - 1, 1)
    g = face(u, f, s, [nxt(x) for x in u], [nxt(x) for x in f], nxt(s))
    out = []
    for k in range(8):
        edge = 0.0 if f[k] is None else f[k] + f[k]
        up = jnp.where(last, edge, g[k])
        out.append(up - jnp.where(first, edge, pltpu.roll(up, 1, 1)))
    return out


def along_y(u, ghost):
    rows = u[0].shape[0]
    ext = [jnp.concatenate([a, b], 0) for a, b in zip(u, ghost)]
    f, s = flux(ext, shared(ext), 1)
    total = ext[0].shape[0]
    nxt = lambda x: None if x is None else jnp.concatenate([x[1:], x[:1]], 0)
    g = face(ext, f, s, [nxt(x) for x in ext], [nxt(x) for x in f], nxt(s))
    return [x[:rows] - jnp.concatenate([x[total - 1 :], x[: rows - 1]], 0) for x in g]


def ghost_rows(lo, hi, l):
    top = lax.broadcasted_iota(jnp.int32, (8, lo.shape[-1]), 0) < 4
    out = []
    for k in range(8):
        a = jnp.broadcast_to(hi[k, l : l + 1, :], top.shape)
        b = jnp.broadcast_to(lo[k, l : l + 1, :], top.shape)
        out.append(jnp.where(top, a, b))
    return out


def kernel(
    n, blocks, d_ref, v_ref, m_ref, p_ref, src_ref, out_ref,
    state, part, lo0, hi0, ysend, ylo, yhi, psend, plo, phi,
    zsend, zlo, zhi, full, full1, mine1, shell, glo, ghi,
    xs, xr, ys, yr, ps, pr, zs, zr, fs, fr, hs, hr,
):
    layers, rows, lanes = d_ref.shape
    end = layers - 1
    corona, helio = blocks // 2, 3 * blocks // 8
    place, sec = lax.axis_index("blk"), lax.axis_index("sec")
    has_lo, has_hi = place > 0, place < blocks - 1
    coupled = (place == corona) | (place == corona + helio)
    source = (place + 1 == corona) | (place + 1 == corona + helio)

    def coeff(at):
        return 0.5 * jnp.where(
            at < corona,
            jnp.float32(0.05),
            jnp.where(at < corona + helio, jnp.float32(0.04), jnp.float32(0.055)),
        )

    c, c_lo, c_hi = coeff(place), coeff(place - 1), coeff(place + 1)
    others = [lax.rem(sec + k, n) for k in range(1, n)]
    north, south = others[0], others[-1]

    def remote(src, dst, s, r, **where):
        return pltpu.make_async_remote_copy(
            src_ref=src, dst_ref=dst, send_sem=s, recv_sem=r, device_id=where, device_id_type=MESH
        )

    def raw_layer(l, dst, s, r, **where):
        remote(d_ref.at[pl.ds(l, 1)], dst.at[pl.ds(0, 1)], s, r, **where).start()
        remote(v_ref.at[:, l], dst.at[pl.ds(1, 3)], s, r, **where).start()
        remote(m_ref.at[:, l], dst.at[pl.ds(4, 3)], s, r, **where).start()
        remote(p_ref.at[pl.ds(l, 1)], dst.at[pl.ds(7, 1)], s, r, **where).start()

    barrier = pltpu.get_barrier_semaphore()

    @pl.when(has_lo)
    def _():
        pl.semaphore_signal(barrier, inc=1, device_id={"blk": place - 1}, device_id_type=MESH)

    @pl.when(has_hi)
    def _():
        pl.semaphore_signal(barrier, inc=1, device_id={"blk": place + 1}, device_id_type=MESH)

    for o in others:
        pl.semaphore_signal(barrier, inc=1, device_id={"sec": o}, device_id_type=MESH)

    def raw(l):
        return (
            [d_ref[l]] + [v_ref[i, l] for i in range(3)] + [m_ref[i, l] for i in range(3)] + [p_ref[l]]
        )

    for l in range(layers):
        for k, x in enumerate(raw(l)):
            ysend[0, k, l : l + 1, :] = x[:1]
            ysend[1, k, l : l + 1, :] = x[rows - 1 :]
    pl.semaphore_wait(
        barrier, n - 1 + has_lo.astype(jnp.int32) + has_hi.astype(jnp.int32)
    )

    @pl.when(has_lo)
    def _():
        raw_layer(0, hi0, xs.at[0], xr.at[0], blk=place - 1)

    @pl.when(has_hi)
    def _():
        raw_layer(end, lo0, xs.at[1], xr.at[1], blk=place + 1)

    y_down = remote(ysend.at[0], yhi, ys.at[0], yr.at[0], sec=south)
    y_up = remote(ysend.at[1], ylo, ys.at[1], yr.at[1], sec=north)
    y_down.start()
    y_up.start()

    @pl.when(source)
    def _():
        for i, o in enumerate(others):
            raw_layer(end, full.at[sec], fs.at[i], fr.at[n - 2 - i], sec=o)
        for k, x in enumerate(raw(end)):
            full[sec, k] = x

    def x_flux(u):
        return flux(u, shared(u), 0)

    def sweep(get, lo_rows, hi_rows, fix, put):
        before = None
        for l in range(layers):
            u = get(l)
            sh = shared(u)
            fx, sx = flux(u, sh, 0)
            total = along_z(u, sh)
            side = along_y(u, fix(ghost_rows(lo_rows, hi_rows, l)))
            total = [a + b for a, b in zip(total, side)]
            if before is not None:
                pu, pf, ps_, ptotal = before
                g = face(pu, pf, ps_, u, fx, sx)
                put(l - 1, pu, [a + b for a, b in zip(ptotal, g)])
                total = [a - b for a, b in zip(total, g)]
            before = (u, fx, sx, total)
        put(end, before[0], before[3])

    def get0(l):
        u = conserve(raw(l))
        for k in range(8):
            state[k, l] = u[k]
        return u

    def put0(l, u, total):
        for k in range(8):
            new = u[k] - c * total[k]
            part[k, l] = new
            if l == 0:
                psend[0, k] = new
            if l == end:
                psend[1, k] = new

    y_down.wait()
    y_up.wait()
    sweep(get0, ylo, yhi, conserve, put0)

    to_lo = remote(psend.at[0], phi, ps.at[0], pr.at[0], blk=place - 1)
    to_hi = remote(psend.at[1], plo, ps.at[1], pr.at[1], blk=place + 1)

    @pl.when(has_lo)
    def _():
        to_lo.start()

    @pl.when(has_hi)
    def _():
        to_hi.start()

    raw_lo = remote(hi0, lo0, xs.at[1], xr.at[1], blk=place + 1)
    raw_hi = remote(lo0, hi0, xs.at[0], xr.at[0], blk=place - 1)

    @pl.when(has_lo)
    def _():
        raw_lo.wait_recv()

    @pl.when(jnp.logical_not(has_lo))
    def _():
        for k, x in enumerate(raw(0)):
            lo0[k] = x

    @pl.when(has_hi)
    def _():
        raw_hi.wait_recv()

    @pl.when(jnp.logical_not(has_hi))
    def _():
        for k, x in enumerate(raw(end)):
            hi0[k] = x

    @pl.when(coupled)
    def _():
        for i, o in enumerate(others):
            remote(lo0, full.at[sec], fs.at[i], fr.at[n - 2 - i], sec=o).start()
        for k in range(8):
            full[sec, k] = lo0[k]

    second = place + 1 >= corona + helio
    index = jnp.where(second, src_ref[1], src_ref[0])
    index_y, index_z = lax.div(index, lanes), lax.rem(index, lanes)

    def gather(ref):
        def body(r, acc):
            here = index_y == r
            s, t = r // rows, r % rows
            new = []
            for k in range(8):
                line = jnp.broadcast_to(ref[s, k, pl.ds(t, 1), :], index.shape)
                got = jnp.take_along_axis(line, index_z, axis=1, mode="promise_in_bounds")
                new.append(jnp.where(here, got, acc[k]))
            return tuple(new)

        zero = jnp.zeros(index.shape, jnp.float32)
        return list(lax.fori_loop(0, n * rows, body, (zero,) * 8))

    @pl.when(coupled | source)
    def _():
        for i in range(n - 1):
            remote(lo0, full.at[others[i]], fs.at[i], fr.at[i], sec=others[i]).wait_recv()
        for k, x in enumerate(gather(full)):
            shell[k] = x

    @pl.when(jnp.logical_not(coupled | source))
    def _():
        for k in range(8):
            shell[k] = lo0[k]

    def load(ref):
        return [ref[k] for k in range(8)]

    def own(l):
        return [state[k, l] for k in range(8)]

    u_lo, u_hi = conserve(load(lo0)), conserve(load(hi0))
    u_sh = conserve(load(shell))
    inner = [jnp.where(coupled, a, b) for a, b in zip(u_sh, u_lo)]
    u0, ue = own(0), own(end)
    f0, s0 = x_flux(u0)
    g_in = face(inner, *x_flux(inner), u0, f0, s0)
    for k in range(8):
        part[k, 0] = part[k, 0] + c * g_in[k]
    fe, se = x_flux(ue)
    fh, sh_ = x_flux(u_hi)
    g_out = face(ue, fe, se, u_hi, fh, sh_)
    for k in range(8):
        part[k, end] = part[k, end] - c * g_out[k]

    for l in range(layers):
        for k in range(8):
            zsend[0, k, l : l + 1, :] = part[k, l, :1, :]
            zsend[1, k, l : l + 1, :] = part[k, l, rows - 1 :, :]
    z_down = remote(zsend.at[0], zhi, zs.at[0], zr.at[0], sec=south)
    z_up = remote(zsend.at[1], zlo, zs.at[1], zr.at[1], sec=north)
    z_down.start()
    z_up.start()

    @pl.when(has_lo)
    def _():
        to_hi.wait_recv()

    @pl.when(has_hi)
    def _():
        to_lo.wait_recv()

    @pl.when(coupled)
    def _():
        low = conserve(load(lo0))
        g = face(low, *x_flux(low), u0, f0, s0)
        for k in range(8):
            new = plo[k] - c_lo * g[k]
            mine1[k] = new
            full1[sec, k] = new
        for i, o in enumerate(others):
            remote(mine1, full1.at[sec], hs.at[i], hr.at[n - 2 - i], sec=o).start()
        for i in range(n - 1):
            remote(mine1, full1.at[others[i]], hs.at[i], hr.at[i], sec=others[i]).wait_recv()
        for k, x in enumerate(gather(full1)):
            glo[k] = x

    @pl.when(jnp.logical_not(has_lo))
    def _():
        for k in range(8):
            glo[k] = part[k, 0]

    @pl.when(has_lo & jnp.logical_not(coupled))
    def _():
        for k in range(8):
            glo[k] = plo[k] - c_lo * g_in[k]

    @pl.when(source)
    def _():
        g = face(u_sh, *x_flux(u_sh), u_hi, fh, sh_)
        for k in range(8):
            ghi[k] = phi[k] + c_hi * g[k]

    @pl.when(jnp.logical_not(has_hi))
    def _():
        for k in range(8):
            ghi[k] = part[k, end]

    @pl.when(has_hi & jnp.logical_not(source))
    def _():
        for k in range(8):
            ghi[k] = phi[k] + c_hi * g_out[k]

    z_down.wait()
    z_up.wait()

    def get1(l):
        return [part[k, l] for k in range(8)]

    def put1(l, u, total):
        if l == 0:
            low = load(glo)
            g = face(low, *x_flux(low), u, *x_flux(u))
            total = [a - b for a, b in zip(total, g)]
        if l == end:
            high = load(ghi)
            g = face(u, *x_flux(u), high, *x_flux(high))
            total = [a + b for a, b in zip(total, g)]
        for k in range(8):
            out_ref[k, l] = u[k] - c * total[k]

    sweep(get1, zlo, zhi, lambda g: g, put1)

    @pl.when(has_lo)
    def _():
        raw_hi.wait_send()
        to_lo.wait_send()

    @pl.when(has_hi)
    def _():
        raw_lo.wait_send()
        to_hi.wait_send()

    @pl.when(coupled | source)
    def _():
        for i, o in enumerate(others):
            remote(lo0, full.at[sec], fs.at[i], fr.at[i], sec=o).wait_send()

    @pl.when(coupled)
    def _():
        for i, o in enumerate(others):
            remote(mine1, full1.at[sec], hs.at[i], hr.at[i], sec=o).wait_send()


def local(density, velocity, magnetic, pressure, shell_source):
    n, blocks = lax.axis_size("sec"), lax.axis_size("blk")
    layers, rows, lanes = density.shape
    vm = lambda *shape: pltpu.VMEM(shape, jnp.float32)
    dma = lambda k: pltpu.SemaphoreType.DMA((k,))
    plane = (8, rows, lanes)
    edge = (8, layers, lanes)
    vmem = pl.BlockSpec(memory_space=pltpu.VMEM)
    return pl.pallas_call(
        functools.partial(kernel, n, blocks),
        out_shape=jax.ShapeDtypeStruct((8,) + density.shape, jnp.float32),
        in_specs=[vmem] * 5,
        out_specs=vmem,
        scratch_shapes=[
            vm(8, layers, rows, lanes), vm(8, layers, rows, lanes),
            vm(*plane), vm(*plane), vm(2, *edge), vm(*edge), vm(*edge),
            vm(2, *plane), vm(*plane), vm(*plane),
            vm(2, *edge), vm(*edge), vm(*edge),
            vm(n, *plane), vm(n, *plane), vm(*plane), vm(*plane), vm(*plane), vm(*plane),
            dma(2), dma(2), dma(2), dma(2), dma(2), dma(2), dma(2), dma(2),
            dma(n - 1), dma(n - 1), dma(n - 1), dma(n - 1),
        ],
        compiler_params=pltpu.CompilerParams(collective_id=0, has_side_effects=True),
    )(density, velocity, magnetic, pressure, shell_source)


def solution(mesh):
    return jax.shard_map(
        local,
        mesh=mesh,
        in_specs=(
            P("blk", "sec", None),
            P(None, "blk", "sec", None),
            P(None, "blk", "sec", None),
            P("blk", "sec", None),
            P(None, "sec", None),
        ),
        out_specs=P(None, "blk", "sec", None),
        check_vma=False,
    )
```

```python
import functools
import jax
import jax.numpy as jnp
from jax import lax
from jax.experimental import pallas as pl
from jax.experimental.pallas import tpu as pltpu
from jax.sharding import PartitionSpec as P

GAMMA = 5.0 / 3.0
MESH = pl.DeviceIdType.MESH


def conserve(raw):
    rho, v, b, p = raw[0], raw[1:4], raw[4:7], raw[7]
    vsq = v[0] * v[0] + v[1] * v[1] + v[2] * v[2]
    bsq = b[0] * b[0] + b[1] * b[1] + b[2] * b[2]
    energy = p * (1.0 / (GAMMA - 1.0)) + 0.5 * rho * vsq + 0.5 * bsq
    return [rho, rho * v[0], rho * v[1], rho * v[2], b[0], b[1], b[2], energy]


def shared(u):
    inv = 1.0 / u[0]
    v = [u[1] * inv, u[2] * inv, u[3] * inv]
    b = u[4:7]
    bsq = b[0] * b[0] + b[1] * b[1] + b[2] * b[2]
    mv = u[1] * v[0] + u[2] * v[1] + u[3] * v[2]
    vb = v[0] * b[0] + v[1] * b[1] + v[2] * b[2]
    half = 0.5 * bsq
    ptot = (GAMMA - 1.0) * (u[7] - 0.5 * mv - half) + half
    fast = jnp.sqrt((GAMMA * (GAMMA - 1.0) * u[7] + bsq) * inv)
    return v, vb, ptot, u[7] + ptot, fast


def flux(u, sh, d):
    v, vb, ptot, ep, fast = sh
    vd, bd = v[d], u[4 + d]
    mom = [u[1 + i] * vd - u[4 + i] * bd for i in range(3)]
    mom[d] = mom[d] + ptot
    ind = [vd * u[4 + i] - bd * v[i] if i != d else None for i in range(3)]
    return [u[1 + d]] + mom + ind + [ep * vd - bd * vb], jnp.abs(vd) + fast


def face(ul, fl, sl, ur, fr, sr):
    reach = jnp.maximum(sl, sr)
    out = []
    for k in range(8):
        jump = reach * (ur[k] - ul[k])
        out.append(-jump if fl[k] is None else (fl[k] + fr[k]) - jump)
    return out


def along_z(u, sh):
    f, s = flux(u, sh, 2)
    lanes = u[0].shape[1]
    lane = lax.broadcasted_iota(jnp.int32, u[0].shape, 1)
    last, first = lane == lanes - 1, lane == 0
    nxt = lambda x: None if x is None else pltpu.roll(x, lanes - 1, 1)
    g = face(u, f, s, [nxt(x) for x in u], [nxt(x) for x in f], nxt(s))
    out = []
    for k in range(8):
        edge = 0.0 if f[k] is None else f[k] + f[k]
        up = jnp.where(last, edge, g[k])
        out.append(up - jnp.where(first, edge, pltpu.roll(up, 1, 1)))
    return out


def along_y(u, ghost):
    rows = u[0].shape[0]
    ext = [jnp.concatenate([a, b], 0) for a, b in zip(u, ghost)]
    f, s = flux(ext, shared(ext), 1)
    total = ext[0].shape[0]
    nxt = lambda x: None if x is None else jnp.concatenate([x[1:], x[:1]], 0)
    g = face(ext, f, s, [nxt(x) for x in ext], [nxt(x) for x in f], nxt(s))
    return [x[:rows] - jnp.concatenate([x[total - 1 :], x[: rows - 1]], 0) for x in g]


def ghost_rows(lo, hi, l):
    top = lax.broadcasted_iota(jnp.int32, (8, lo.shape[-1]), 0) < 4
    out = []
    for k in range(8):
        a = jnp.broadcast_to(hi[k, l : l + 1, :], top.shape)
        b = jnp.broadcast_to(lo[k, l : l + 1, :], top.shape)
        out.append(jnp.where(top, a, b))
    return out


def kernel(
    n, blocks, d_in, v_in, m_in, p_in, src_in, out_ref,
    d_ref, v_ref, m_ref, p_ref, src_ref, loads,
    state, part, lo0, hi0, ysend, ylo, yhi, psend, plo, phi,
    zsend, zlo, zhi, full, full1, ghost, shell, glo, ghi,
    xs, xr, ys, yr, ps, pr, zs, zr, fs, fr, hs, hr,
):
    layers, rows, lanes = d_ref.shape
    end = layers - 1
    corona, helio = blocks // 2, 3 * blocks // 8
    place, sec = lax.axis_index("blk"), lax.axis_index("sec")
    has_lo, has_hi = place > 0, place < blocks - 1
    coupled = (place == corona) | (place == corona + helio)
    source = (place + 1 == corona) | (place + 1 == corona + helio)

    def coeff(at):
        return 0.5 * jnp.where(
            at < corona,
            jnp.float32(0.05),
            jnp.where(at < corona + helio, jnp.float32(0.04), jnp.float32(0.055)),
        )

    c, c_lo, c_hi = coeff(place), coeff(place - 1), coeff(place + 1)
    others = [lax.rem(sec + k, n) for k in range(1, n)]
    north, south = others[0], others[-1]

    def remote(src, dst, s, r, **where):
        return pltpu.make_async_remote_copy(
            src_ref=src, dst_ref=dst, send_sem=s, recv_sem=r, device_id=where, device_id_type=MESH
        )

    def raw_layer(l, dst, s, r, **where):
        remote(d_in.at[pl.ds(l, 1)], dst.at[pl.ds(0, 1)], s, r, **where).start()
        remote(v_in.at[:, l], dst.at[pl.ds(1, 3)], s, r, **where).start()
        remote(m_in.at[:, l], dst.at[pl.ds(4, 3)], s, r, **where).start()
        remote(p_in.at[pl.ds(l, 1)], dst.at[pl.ds(7, 1)], s, r, **where).start()

    pairs = ((d_in, d_ref), (v_in, v_ref), (m_in, m_ref), (p_in, p_ref), (src_in, src_ref))
    reads = [pltpu.make_async_copy(a, b, loads.at[i]) for i, (a, b) in enumerate(pairs)]
    for read in reads:
        read.start()
    barrier = pltpu.get_barrier_semaphore()

    @pl.when(has_lo)
    def _():
        pl.semaphore_signal(barrier, inc=1, device_id={"blk": place - 1}, device_id_type=MESH)

    @pl.when(has_hi)
    def _():
        pl.semaphore_signal(barrier, inc=1, device_id={"blk": place + 1}, device_id_type=MESH)

    for o in others:
        pl.semaphore_signal(barrier, inc=1, device_id={"sec": o}, device_id_type=MESH)

    def raw(l):
        return (
            [d_ref[l]] + [v_ref[i, l] for i in range(3)] + [m_ref[i, l] for i in range(3)] + [p_ref[l]]
        )

    for read in reads:
        read.wait()
    for l in range(layers):
        for k, x in enumerate(raw(l)):
            ysend[0, k, l : l + 1, :] = x[:1]
            ysend[1, k, l : l + 1, :] = x[rows - 1 :]
    pl.semaphore_wait(
        barrier, n - 1 + has_lo.astype(jnp.int32) + has_hi.astype(jnp.int32)
    )

    @pl.when(has_lo)
    def _():
        raw_layer(0, hi0, xs.at[0], xr.at[0], blk=place - 1)

    @pl.when(has_hi)
    def _():
        raw_layer(end, lo0, xs.at[1], xr.at[1], blk=place + 1)

    y_down = remote(ysend.at[0], yhi, ys.at[0], yr.at[0], sec=south)
    y_up = remote(ysend.at[1], ylo, ys.at[1], yr.at[1], sec=north)
    y_down.start()
    y_up.start()

    @pl.when(source)
    def _():
        for i, o in enumerate(others):
            raw_layer(end, full.at[sec], fs.at[i], fr.at[n - 2 - i], sec=o)
        for k, x in enumerate(raw(end)):
            full[sec, k] = x

    def x_flux(u):
        return flux(u, shared(u), 0)

    def sweep(get, put):
        before = None
        for l in range(layers):
            u = get(l)
            sh = shared(u)
            fx, sx = flux(u, sh, 0)
            total = along_z(u, sh)
            if before is not None:
                pu, pf, ps_, ptotal = before
                g = face(pu, pf, ps_, u, fx, sx)
                put(l - 1, pu, [a + b for a, b in zip(ptotal, g)])
                total = [a - b for a, b in zip(total, g)]
            before = (u, fx, sx, total)
        put(end, before[0], before[3])

    def get0(l):
        u = conserve(raw(l))
        for k in range(8):
            state[k, l] = u[k]
        return u

    def put0(l, u, total):
        for k in range(8):
            part[k, l] = u[k] - c * total[k]

    sweep(get0, put0)
    y_down.wait()
    y_up.wait()
    for l in [0, end] + list(range(1, end)):
        u = [state[k, l] for k in range(8)]
        side = along_y(u, conserve(ghost_rows(ylo, yhi, l)))
        for k in range(8):
            new = part[k, l] - c * side[k]
            part[k, l] = new
            if l == 0:
                psend[0, k] = new
            if l == end:
                psend[1, k] = new

    to_lo = remote(psend.at[0], phi, ps.at[0], pr.at[0], blk=place - 1)
    to_hi = remote(psend.at[1], plo, ps.at[1], pr.at[1], blk=place + 1)

    @pl.when(has_lo)
    def _():
        to_lo.start()

    @pl.when(has_hi)
    def _():
        to_hi.start()

    raw_lo = remote(hi0, lo0, xs.at[1], xr.at[1], blk=place + 1)
    raw_hi = remote(lo0, hi0, xs.at[0], xr.at[0], blk=place - 1)

    @pl.when(has_lo)
    def _():
        raw_lo.wait_recv()

    @pl.when(jnp.logical_not(has_lo))
    def _():
        for k, x in enumerate(raw(0)):
            lo0[k] = x

    @pl.when(has_hi)
    def _():
        raw_hi.wait_recv()

    @pl.when(jnp.logical_not(has_hi))
    def _():
        for k, x in enumerate(raw(end)):
            hi0[k] = x

    @pl.when(coupled)
    def _():
        for i, o in enumerate(others):
            remote(lo0, full.at[sec], fs.at[i], fr.at[n - 2 - i], sec=o).start()
        for k in range(8):
            full[sec, k] = lo0[k]

    second = place + 1 >= corona + helio
    index = jnp.where(second, src_ref[1], src_ref[0])
    index_y, index_z = lax.div(index, lanes), lax.rem(index, lanes)

    def gather(ref, s, acc):
        def body(t, acc):
            here = index_y == s * rows + t
            new = []
            for k in range(8):
                line = jnp.broadcast_to(ref[s, k, pl.ds(t, 1), :], index.shape)
                got = jnp.take_along_axis(line, index_z, axis=1, mode="promise_in_bounds")
                new.append(jnp.where(here, got, acc[k]))
            return tuple(new)

        return lax.fori_loop(0, rows, body, acc, unroll=8)

    def gather_all(ref, arrived):
        acc = gather(ref, sec, (jnp.zeros(index.shape, jnp.float32),) * 8)
        for i in range(n - 1):
            arrived(i).wait_recv()
            acc = gather(ref, others[i], acc)
        return acc

    def load(ref):
        return [ref[k] for k in range(8)]

    def own(l):
        return [state[k, l] for k in range(8)]

    u_lo, u_hi = conserve(load(lo0)), conserve(load(hi0))
    u0, ue = own(0), own(end)
    f0, s0 = x_flux(u0)
    fl_, sl_ = x_flux(u_lo)
    g_true = face(u_lo, fl_, sl_, u0, f0, s0)
    fe, se = x_flux(ue)
    fh, sh_ = x_flux(u_hi)
    g_out = face(ue, fe, se, u_hi, fh, sh_)
    for k in range(8):
        part[k, end] = part[k, end] - c * g_out[k]

    @pl.when(has_lo)
    def _():
        to_hi.wait_recv()
        for k in range(8):
            glo[k] = plo[k] - c_lo * g_true[k]

    @pl.when(coupled)
    def _():
        for k in range(8):
            full1[sec, k] = glo[k]
        for i, o in enumerate(others):
            remote(glo, full1.at[sec], hs.at[i], hr.at[n - 2 - i], sec=o).start()

    @pl.when(coupled | source)
    def _():
        arrived = lambda i: remote(lo0, full.at[others[i]], fs.at[i], fr.at[i], sec=others[i])
        for k, x in enumerate(gather_all(full, arrived)):
            shell[k] = x

    @pl.when(jnp.logical_not(coupled | source))
    def _():
        for k in range(8):
            shell[k] = lo0[k]

    u_sh = conserve(load(shell))
    inner = [jnp.where(coupled, a, b) for a, b in zip(u_sh, u_lo)]
    g_in = face(inner, *x_flux(inner), u0, f0, s0)
    for k in range(8):
        part[k, 0] = part[k, 0] + c * g_in[k]

    def load(ref):
        return [ref[k] for k in range(8)]

    def own(l):
        return [state[k, l] for k in range(8)]

    for l in range(layers):
        for k in range(8):
            zsend[0, k, l : l + 1, :] = part[k, l, :1, :]
            zsend[1, k, l : l + 1, :] = part[k, l, rows - 1 :, :]
    z_down = remote(zsend.at[0], zhi, zs.at[0], zr.at[0], sec=south)
    z_up = remote(zsend.at[1], zlo, zs.at[1], zr.at[1], sec=north)
    z_down.start()
    z_up.start()

    @pl.when(has_hi)
    def _():
        to_lo.wait_recv()

    @pl.when(coupled)
    def _():
        arrived = lambda i: remote(glo, full1.at[others[i]], hs.at[i], hr.at[i], sec=others[i])
        for k, x in enumerate(gather_all(full1, arrived)):
            ghost[k] = x

    @pl.when(jnp.logical_not(has_lo))
    def _():
        for k in range(8):
            ghost[k] = part[k, 0]

    @pl.when(has_lo & jnp.logical_not(coupled))
    def _():
        for k in range(8):
            ghost[k] = glo[k]

    @pl.when(source)
    def _():
        g = face(u_sh, *x_flux(u_sh), u_hi, fh, sh_)
        for k in range(8):
            ghi[k] = phi[k] + c_hi * g[k]

    @pl.when(jnp.logical_not(has_hi))
    def _():
        for k in range(8):
            ghi[k] = part[k, end]

    @pl.when(has_hi & jnp.logical_not(source))
    def _():
        for k in range(8):
            ghi[k] = phi[k] + c_hi * g_out[k]

    def get1(l):
        return [part[k, l] for k in range(8)]

    def put1(l, u, total):
        if l == 0:
            low = load(ghost)
            g = face(low, *x_flux(low), u, *x_flux(u))
            total = [a - b for a, b in zip(total, g)]
        if l == end:
            high = load(ghi)
            g = face(u, *x_flux(u), high, *x_flux(high))
            total = [a + b for a, b in zip(total, g)]
        for k in range(8):
            state[k, l] = u[k] - c * total[k]

    sweep(get1, put1)
    z_down.wait()
    z_up.wait()
    for l in range(layers):
        side = along_y(get1(l), ghost_rows(zlo, zhi, l))
        for k in range(8):
            out_ref[k, l] = state[k, l] - c * side[k]

    @pl.when(has_lo)
    def _():
        raw_hi.wait_send()
        to_lo.wait_send()

    @pl.when(has_hi)
    def _():
        raw_lo.wait_send()
        to_hi.wait_send()

    @pl.when(coupled | source)
    def _():
        for i, o in enumerate(others):
            remote(lo0, full.at[sec], fs.at[i], fr.at[i], sec=o).wait_send()

    @pl.when(coupled)
    def _():
        for i, o in enumerate(others):
            remote(glo, full1.at[sec], hs.at[i], hr.at[i], sec=o).wait_send()


def local(density, velocity, magnetic, pressure, shell_source):
    n, blocks = lax.axis_size("sec"), lax.axis_size("blk")
    layers, rows, lanes = density.shape
    vm = lambda *shape: pltpu.VMEM(shape, jnp.float32)
    dma = lambda k: pltpu.SemaphoreType.DMA((k,))
    plane = (8, rows, lanes)
    edge = (8, layers, lanes)
    vmem = pl.BlockSpec(memory_space=pltpu.VMEM)
    hold = lambda x: pltpu.with_memory_space_constraint(x, pltpu.HBM)
    return pl.pallas_call(
        functools.partial(kernel, n, blocks),
        out_shape=jax.ShapeDtypeStruct((8,) + density.shape, jnp.float32),
        in_specs=[pl.BlockSpec(memory_space=pltpu.HBM)] * 5,
        out_specs=vmem,
        scratch_shapes=[
            vm(layers, rows, lanes), vm(3, layers, rows, lanes), vm(3, layers, rows, lanes),
            vm(layers, rows, lanes), pltpu.VMEM(shell_source.shape, jnp.int32), dma(5),
            vm(8, layers, rows, lanes), vm(8, layers, rows, lanes),
            vm(*plane), vm(*plane), vm(2, *edge), vm(*edge), vm(*edge),
            vm(2, *plane), vm(*plane), vm(*plane),
            vm(2, *edge), vm(*edge), vm(*edge),
            vm(n, *plane), vm(n, *plane), vm(*plane), vm(*plane), vm(*plane), vm(*plane),
            dma(2), dma(2), dma(2), dma(2), dma(2), dma(2), dma(2), dma(2),
            dma(n - 1), dma(n - 1), dma(n - 1), dma(n - 1),
        ],
        compiler_params=pltpu.CompilerParams(vmem_limit_bytes=8 * 2**20, collective_id=0, has_side_effects=True),
    )(*map(hold, (density, velocity, magnetic, pressure, shell_source)))


def solution(mesh):
    return jax.shard_map(
        local,
        mesh=mesh,
        in_specs=(
            P("blk", "sec", None),
            P(None, "blk", "sec", None),
            P(None, "blk", "sec", None),
            P("blk", "sec", None),
            P(None, "sec", None),
        ),
        out_specs=P(None, "blk", "sec", None),
        check_vma=False,
    )
```

```python
import functools
import jax
import jax.numpy as jnp
from jax import lax
from jax.experimental import pallas as pl
from jax.experimental.pallas import tpu as pltpu
from jax.sharding import PartitionSpec as P

GAMMA = 5.0 / 3.0
MESH = pl.DeviceIdType.MESH


def conserve(raw):
    rho, v, b, p = raw[0], raw[1:4], raw[4:7], raw[7]
    vsq = v[0] * v[0] + v[1] * v[1] + v[2] * v[2]
    bsq = b[0] * b[0] + b[1] * b[1] + b[2] * b[2]
    energy = p * (1.0 / (GAMMA - 1.0)) + 0.5 * rho * vsq + 0.5 * bsq
    return [rho, rho * v[0], rho * v[1], rho * v[2], b[0], b[1], b[2], energy]


def shared(u):
    inv = 1.0 / u[0]
    v = [u[1] * inv, u[2] * inv, u[3] * inv]
    b = u[4:7]
    bsq = b[0] * b[0] + b[1] * b[1] + b[2] * b[2]
    mv = u[1] * v[0] + u[2] * v[1] + u[3] * v[2]
    vb = v[0] * b[0] + v[1] * b[1] + v[2] * b[2]
    half = 0.5 * bsq
    ptot = (GAMMA - 1.0) * (u[7] - 0.5 * mv - half) + half
    fast = jnp.sqrt((GAMMA * (GAMMA - 1.0) * u[7] + bsq) * inv)
    return v, vb, ptot, u[7] + ptot, fast


def flux(u, sh, d):
    v, vb, ptot, ep, fast = sh
    vd, bd = v[d], u[4 + d]
    mom = [u[1 + i] * vd - u[4 + i] * bd for i in range(3)]
    mom[d] = mom[d] + ptot
    ind = [vd * u[4 + i] - bd * v[i] if i != d else None for i in range(3)]
    return [u[1 + d]] + mom + ind + [ep * vd - bd * vb], jnp.abs(vd) + fast


def face(ul, fl, sl, ur, fr, sr):
    reach = jnp.maximum(sl, sr)
    out = []
    for k in range(8):
        jump = reach * (ur[k] - ul[k])
        out.append(-jump if fl[k] is None else (fl[k] + fr[k]) - jump)
    return out


def along_z(u, sh):
    f, s = flux(u, sh, 2)
    lanes = u[0].shape[1]
    lane = lax.broadcasted_iota(jnp.int32, u[0].shape, 1)
    last, first = lane == lanes - 1, lane == 0
    nxt = lambda x: None if x is None else pltpu.roll(x, lanes - 1, 1)
    g = face(u, f, s, [nxt(x) for x in u], [nxt(x) for x in f], nxt(s))
    out = []
    for k in range(8):
        edge = 0.0 if f[k] is None else f[k] + f[k]
        up = jnp.where(last, edge, g[k])
        out.append(up - jnp.where(first, edge, pltpu.roll(up, 1, 1)))
    return out


def along_y(u, ghost):
    rows = u[0].shape[0]
    ext = [jnp.concatenate([a, b], 0) for a, b in zip(u, ghost)]
    f, s = flux(ext, shared(ext), 1)
    total = ext[0].shape[0]
    nxt = lambda x: None if x is None else jnp.concatenate([x[1:], x[:1]], 0)
    g = face(ext, f, s, [nxt(x) for x in ext], [nxt(x) for x in f], nxt(s))
    return [x[:rows] - jnp.concatenate([x[total - 1 :], x[: rows - 1]], 0) for x in g]


def ghost_rows(lo, hi, l):
    top = lax.broadcasted_iota(jnp.int32, (8, lo.shape[-1]), 0) < 4
    out = []
    for k in range(8):
        a = jnp.broadcast_to(hi[k, l : l + 1, :], top.shape)
        b = jnp.broadcast_to(lo[k, l : l + 1, :], top.shape)
        out.append(jnp.where(top, a, b))
    return out


def kernel(
    n, blocks, d_in, v_in, m_in, p_in, src_in, out_ref,
    d_ref, v_ref, m_ref, p_ref, src_ref, loads,
    state, part, lo0, hi0, ysend, ylo, yhi, psend, plo, phi,
    zsend, zlo, zhi, full, full1, ghost, shell, glo, ghi, edges,
    xs, xr, ys, yr, ps, pr, zs, zr, fs, fr, hs, hr,
):
    layers, rows, lanes = d_ref.shape
    end = layers - 1
    corona, helio = blocks // 2, 3 * blocks // 8
    place, sec = lax.axis_index("blk"), lax.axis_index("sec")
    has_lo, has_hi = place > 0, place < blocks - 1
    coupled = (place == corona) | (place == corona + helio)
    source = (place + 1 == corona) | (place + 1 == corona + helio)

    def coeff(at):
        return 0.5 * jnp.where(
            at < corona,
            jnp.float32(0.05),
            jnp.where(at < corona + helio, jnp.float32(0.04), jnp.float32(0.055)),
        )

    c, c_lo, c_hi = coeff(place), coeff(place - 1), coeff(place + 1)
    others = [lax.rem(sec + k, n) for k in range(1, n)]
    north, south = others[0], others[-1]

    def remote(src, dst, s, r, **where):
        return pltpu.make_async_remote_copy(
            src_ref=src, dst_ref=dst, send_sem=s, recv_sem=r, device_id=where, device_id_type=MESH
        )

    def raw_layer(l, dst, s, r, **where):
        remote(d_in.at[pl.ds(l, 1)], dst.at[pl.ds(0, 1)], s, r, **where).start()
        remote(v_in.at[:, l], dst.at[pl.ds(1, 3)], s, r, **where).start()
        remote(m_in.at[:, l], dst.at[pl.ds(4, 3)], s, r, **where).start()
        remote(p_in.at[pl.ds(l, 1)], dst.at[pl.ds(7, 1)], s, r, **where).start()

    pairs = ((d_in, d_ref), (v_in, v_ref), (m_in, m_ref), (p_in, p_ref), (src_in, src_ref))
    reads = [pltpu.make_async_copy(a, b, loads.at[i]) for i, (a, b) in enumerate(pairs)]
    for read in reads:
        read.start()
    barrier = pltpu.get_barrier_semaphore()

    @pl.when(has_lo)
    def _():
        pl.semaphore_signal(barrier, inc=1, device_id={"blk": place - 1}, device_id_type=MESH)

    @pl.when(has_hi)
    def _():
        pl.semaphore_signal(barrier, inc=1, device_id={"blk": place + 1}, device_id_type=MESH)

    for o in others:
        pl.semaphore_signal(barrier, inc=1, device_id={"sec": o}, device_id_type=MESH)

    def raw(l):
        return (
            [d_ref[l]] + [v_ref[i, l] for i in range(3)] + [m_ref[i, l] for i in range(3)] + [p_ref[l]]
        )

    for read in reads:
        read.wait()
    for l in range(layers):
        for k, x in enumerate(raw(l)):
            ysend[0, k, l : l + 1, :] = x[:1]
            ysend[1, k, l : l + 1, :] = x[rows - 1 :]
    pl.semaphore_wait(
        barrier, n - 1 + has_lo.astype(jnp.int32) + has_hi.astype(jnp.int32)
    )

    @pl.when(has_lo)
    def _():
        raw_layer(0, hi0, xs.at[0], xr.at[0], blk=place - 1)

    @pl.when(has_hi)
    def _():
        raw_layer(end, lo0, xs.at[1], xr.at[1], blk=place + 1)

    y_down = remote(ysend.at[0], yhi, ys.at[0], yr.at[0], sec=south)
    y_up = remote(ysend.at[1], ylo, ys.at[1], yr.at[1], sec=north)
    y_down.start()
    y_up.start()

    @pl.when(source)
    def _():
        for i, o in enumerate(others):
            raw_layer(end, full.at[sec], fs.at[i], fr.at[n - 2 - i], sec=o)
        for k, x in enumerate(raw(end)):
            full[sec, k] = x

    def x_flux(u):
        return flux(u, shared(u), 0)

    def keep(i, f, s):
        for k in range(8):
            if f[k] is not None:
                edges[i, k] = f[k]
        edges[i, 4] = s

    def kept(i):
        return [edges[i, k] if k != 4 else None for k in range(8)], edges[i, 4]

    def sweep(get, put):
        before = None
        for l in range(layers):
            u = get(l)
            sh = shared(u)
            fx, sx = flux(u, sh, 0)
            total = along_z(u, sh)
            if before is not None:
                pu, pf, ps_, ptotal = before
                g = face(pu, pf, ps_, u, fx, sx)
                put(l - 1, pu, [a + b for a, b in zip(ptotal, g)])
                total = [a - b for a, b in zip(total, g)]
            before = (u, fx, sx, total)
        put(end, before[0], before[3])

    def get0(l):
        u = conserve(raw(l))
        for k in range(8):
            state[k, l] = u[k]
        return u

    def put0(l, u, total):
        for k in range(8):
            part[k, l] = u[k] - c * total[k]

    sweep(get0, put0)
    y_down.wait()
    y_up.wait()
    for l in [0, end] + list(range(1, end)):
        u = [state[k, l] for k in range(8)]
        side = along_y(u, conserve(ghost_rows(ylo, yhi, l)))
        for k in range(8):
            new = part[k, l] - c * side[k]
            part[k, l] = new
            if l == 0:
                psend[0, k] = new
            if l == end:
                psend[1, k] = new

    to_lo = remote(psend.at[0], phi, ps.at[0], pr.at[0], blk=place - 1)
    to_hi = remote(psend.at[1], plo, ps.at[1], pr.at[1], blk=place + 1)

    @pl.when(has_lo)
    def _():
        to_lo.start()

    @pl.when(has_hi)
    def _():
        to_hi.start()

    middle = list(range(1, end))
    before = None
    for l in middle:
        u = [part[k, l] for k in range(8)]
        sh = shared(u)
        fx, sx = flux(u, sh, 0)
        total = along_z(u, sh)
        if l == middle[0]:
            keep(0, fx, sx)
        if l == middle[-1]:
            keep(1, fx, sx)
        if before is not None:
            pu, pf, ps_, ptotal = before
            g = face(pu, pf, ps_, u, fx, sx)
            for k in range(8):
                state[k, l - 1] = ptotal[k] + g[k]
            total = [a - b for a, b in zip(total, g)]
        before = (u, fx, sx, total)
    for k in range(8):
        state[k, middle[-1]] = before[3][k]

    raw_lo = remote(hi0, lo0, xs.at[1], xr.at[1], blk=place + 1)
    raw_hi = remote(lo0, hi0, xs.at[0], xr.at[0], blk=place - 1)

    @pl.when(has_lo)
    def _():
        raw_lo.wait_recv()

    @pl.when(jnp.logical_not(has_lo))
    def _():
        for k, x in enumerate(raw(0)):
            lo0[k] = x

    @pl.when(coupled)
    def _():
        for i, o in enumerate(others):
            remote(lo0, full.at[sec], fs.at[i], fr.at[n - 2 - i], sec=o).start()
        for k in range(8):
            full[sec, k] = lo0[k]

    @pl.when(has_hi)
    def _():
        raw_hi.wait_recv()

    @pl.when(jnp.logical_not(has_hi))
    def _():
        for k, x in enumerate(raw(end)):
            hi0[k] = x

    second = place + 1 >= corona + helio
    index = jnp.where(second, src_ref[1], src_ref[0])
    index_y, index_z = lax.div(index, lanes), lax.rem(index, lanes)

    def gather(ref, s, acc):
        def body(t, acc):
            here = index_y == s * rows + t
            new = []
            for k in range(8):
                line = jnp.broadcast_to(ref[s, k, pl.ds(t, 1), :], index.shape)
                got = jnp.take_along_axis(line, index_z, axis=1, mode="promise_in_bounds")
                new.append(jnp.where(here, got, acc[k]))
            return tuple(new)

        return lax.fori_loop(0, rows, body, acc, unroll=8)

    def gather_all(ref, arrived):
        acc = gather(ref, sec, (jnp.zeros(index.shape, jnp.float32),) * 8)
        for i in range(n - 1):
            arrived(i).wait_recv()
            acc = gather(ref, others[i], acc)
        return acc

    def load(ref):
        return [ref[k] for k in range(8)]

    def own(l):
        return [state[k, l] for k in range(8)]

    arrived0 = lambda i: remote(lo0, full.at[others[i]], fs.at[i], fr.at[i], sec=others[i])
    arrived1 = lambda i: remote(glo, full1.at[others[i]], hs.at[i], hr.at[i], sec=others[i])

    u_lo, u_hi = conserve(load(lo0)), conserve(load(hi0))
    u0, ue = own(0), own(end)
    f0, s0 = x_flux(u0)
    fe, se = x_flux(ue)
    fh, sh_ = x_flux(u_hi)
    g_out = face(ue, fe, se, u_hi, fh, sh_)
    g_true = face(u_lo, *x_flux(u_lo), u0, f0, s0)
    for k in range(8):
        part[k, end] = part[k, end] - c * g_out[k]
        shell[k] = g_true[k]

    @pl.when(coupled)
    def _():
        inner = conserve(gather_all(full, arrived0))
        for k, x in enumerate(face(inner, *x_flux(inner), u0, f0, s0)):
            shell[k] = x

    for k in range(8):
        part[k, 0] = part[k, 0] + c * shell[k]
    for l in range(layers):
        for k in range(8):
            zsend[0, k, l : l + 1, :] = part[k, l, :1, :]
            zsend[1, k, l : l + 1, :] = part[k, l, rows - 1 :, :]
    z_down = remote(zsend.at[0], zhi, zs.at[0], zr.at[0], sec=south)
    z_up = remote(zsend.at[1], zlo, zs.at[1], zr.at[1], sec=north)
    z_down.start()
    z_up.start()

    @pl.when(coupled)
    def _():
        to_hi.wait_recv()
        for k in range(8):
            new = plo[k] - c_lo * g_true[k]
            glo[k] = new
            full1[sec, k] = new
        for i, o in enumerate(others):
            remote(glo, full1.at[sec], hs.at[i], hr.at[n - 2 - i], sec=o).start()

    for k in range(8):
        ghi[k] = g_out[k]

    @pl.when(source)
    def _():
        low = conserve(gather_all(full, arrived0))
        for k, x in enumerate(face(low, *x_flux(low), u_hi, fh, sh_)):
            ghi[k] = x

    def get1(l):
        return [part[k, l] for k in range(8)]

    v0, ve = get1(0), get1(end)
    h0, he = shared(v0), shared(ve)
    p0, q0 = flux(v0, h0, 0)
    pe, qe = flux(ve, he, 0)
    below = face(v0, p0, q0, get1(1), *kept(0))
    above = face(get1(end - 1), *kept(1), ve, pe, qe)
    z0, ze = along_z(v0, h0), along_z(ve, he)
    for k in range(8):
        state[k, 0] = z0[k] + below[k]
        state[k, end] = ze[k] - above[k]
        state[k, 1] = state[k, 1] - below[k]
        state[k, end - 1] = state[k, end - 1] + above[k]
    z_down.wait()
    z_up.wait()
    for l in [0, end] + middle:
        side = along_y(get1(l), ghost_rows(zlo, zhi, l))
        for k in range(8):
            if l in middle:
                out_ref[k, l] = part[k, l] - c * (state[k, l] + side[k])
            else:
                state[k, l] = state[k, l] + side[k]

    @pl.when(has_hi)
    def _():
        to_lo.wait_recv()
        for k in range(8):
            ghi[k] = phi[k] + c_hi * ghi[k]

    @pl.when(jnp.logical_not(has_hi))
    def _():
        for k in range(8):
            ghi[k] = part[k, end]

    @pl.when(jnp.logical_not(has_lo))
    def _():
        for k in range(8):
            ghost[k] = part[k, 0]

    @pl.when(has_lo & jnp.logical_not(coupled))
    def _():
        to_hi.wait_recv()
        for k in range(8):
            ghost[k] = plo[k] - c_lo * shell[k]

    @pl.when(coupled)
    def _():
        for k, x in enumerate(gather_all(full1, arrived1)):
            ghost[k] = x

    low, high = load(ghost), load(ghi)
    g_low = face(low, *x_flux(low), v0, p0, q0)
    g_high = face(ve, pe, qe, high, *x_flux(high))
    for k in range(8):
        out_ref[k, 0] = v0[k] - c * (state[k, 0] - g_low[k])
        out_ref[k, end] = ve[k] - c * (state[k, end] + g_high[k])

    @pl.when(has_lo)
    def _():
        raw_hi.wait_send()
        to_lo.wait_send()

    @pl.when(has_hi)
    def _():
        raw_lo.wait_send()
        to_hi.wait_send()

    @pl.when(coupled | source)
    def _():
        for i, o in enumerate(others):
            remote(lo0, full.at[sec], fs.at[i], fr.at[i], sec=o).wait_send()

    @pl.when(coupled)
    def _():
        for i, o in enumerate(others):
            remote(glo, full1.at[sec], hs.at[i], hr.at[i], sec=o).wait_send()


def local(density, velocity, magnetic, pressure, shell_source):
    n, blocks = lax.axis_size("sec"), lax.axis_size("blk")
    layers, rows, lanes = density.shape
    vm = lambda *shape: pltpu.VMEM(shape, jnp.float32)
    dma = lambda k: pltpu.SemaphoreType.DMA((k,))
    plane = (8, rows, lanes)
    edge = (8, layers, lanes)
    vmem = pl.BlockSpec(memory_space=pltpu.VMEM)
    hold = lambda x: pltpu.with_memory_space_constraint(x, pltpu.HBM)
    return pl.pallas_call(
        functools.partial(kernel, n, blocks),
        out_shape=jax.ShapeDtypeStruct((8,) + density.shape, jnp.float32),
        in_specs=[pl.BlockSpec(memory_space=pltpu.HBM)] * 5,
        out_specs=vmem,
        scratch_shapes=[
            vm(layers, rows, lanes), vm(3, layers, rows, lanes), vm(3, layers, rows, lanes),
            vm(layers, rows, lanes), pltpu.VMEM(shell_source.shape, jnp.int32), dma(5),
            vm(8, layers, rows, lanes), vm(8, layers, rows, lanes),
            vm(*plane), vm(*plane), vm(2, *edge), vm(*edge), vm(*edge),
            vm(2, *plane), vm(*plane), vm(*plane),
            vm(2, *edge), vm(*edge), vm(*edge),
            vm(n, *plane), vm(n, *plane), vm(*plane), vm(*plane), vm(*plane), vm(*plane), vm(2, *plane),
            dma(2), dma(2), dma(2), dma(2), dma(2), dma(2), dma(2), dma(2),
            dma(n - 1), dma(n - 1), dma(n - 1), dma(n - 1),
        ],
        compiler_params=pltpu.CompilerParams(vmem_limit_bytes=8 * 2**20, collective_id=0, has_side_effects=True),
    )(*map(hold, (density, velocity, magnetic, pressure, shell_source)))


def solution(mesh):
    return jax.shard_map(
        local,
        mesh=mesh,
        in_specs=(
            P("blk", "sec", None),
            P(None, "blk", "sec", None),
            P(None, "blk", "sec", None),
            P("blk", "sec", None),
            P(None, "sec", None),
        ),
        out_specs=P(None, "blk", "sec", None),
        check_vma=False,
    )
```

```python
import functools
import jax
import jax.numpy as jnp
from jax import lax
from jax.experimental import pallas as pl
from jax.experimental.pallas import tpu as pltpu
from jax.sharding import PartitionSpec as P

GAMMA = 5.0 / 3.0
MESH = pl.DeviceIdType.MESH


def conserve(raw):
    rho, v, b, p = raw[0], raw[1:4], raw[4:7], raw[7]
    vsq = v[0] * v[0] + v[1] * v[1] + v[2] * v[2]
    bsq = b[0] * b[0] + b[1] * b[1] + b[2] * b[2]
    energy = p * (1.0 / (GAMMA - 1.0)) + 0.5 * rho * vsq + 0.5 * bsq
    return [rho, rho * v[0], rho * v[1], rho * v[2], b[0], b[1], b[2], energy]


def shared(u):
    inv = 1.0 / u[0]
    v = [u[1] * inv, u[2] * inv, u[3] * inv]
    b = u[4:7]
    bsq = b[0] * b[0] + b[1] * b[1] + b[2] * b[2]
    mv = u[1] * v[0] + u[2] * v[1] + u[3] * v[2]
    vb = v[0] * b[0] + v[1] * b[1] + v[2] * b[2]
    half = 0.5 * bsq
    ptot = (GAMMA - 1.0) * (u[7] - 0.5 * mv - half) + half
    fast = jnp.sqrt((GAMMA * (GAMMA - 1.0) * u[7] + bsq) * inv)
    return v, vb, ptot, u[7] + ptot, fast


def flux(u, sh, d):
    v, vb, ptot, ep, fast = sh
    vd, bd = v[d], u[4 + d]
    mom = [u[1 + i] * vd - u[4 + i] * bd for i in range(3)]
    mom[d] = mom[d] + ptot
    ind = [vd * u[4 + i] - bd * v[i] if i != d else None for i in range(3)]
    return [u[1 + d]] + mom + ind + [ep * vd - bd * vb], jnp.abs(vd) + fast


def face(ul, fl, sl, ur, fr, sr):
    reach = jnp.maximum(sl, sr)
    out = []
    for k in range(8):
        jump = reach * (ur[k] - ul[k])
        out.append(-jump if fl[k] is None else (fl[k] + fr[k]) - jump)
    return out


def along_z(u, sh):
    f, s = flux(u, sh, 2)
    lanes = u[0].shape[1]
    lane = lax.broadcasted_iota(jnp.int32, u[0].shape, 1)
    last, first = lane == lanes - 1, lane == 0
    nxt = lambda x: None if x is None else pltpu.roll(x, lanes - 1, 1)
    g = face(u, f, s, [nxt(x) for x in u], [nxt(x) for x in f], nxt(s))
    out = []
    for k in range(8):
        edge = 0.0 if f[k] is None else f[k] + f[k]
        up = jnp.where(last, edge, g[k])
        out.append(up - jnp.where(first, edge, pltpu.roll(up, 1, 1)))
    return out


def along_y(u, ghost):
    rows = u[0].shape[0]
    ext = [jnp.concatenate([a, b], 0) for a, b in zip(u, ghost)]
    f, s = flux(ext, shared(ext), 1)
    total = ext[0].shape[0]
    nxt = lambda x: None if x is None else jnp.concatenate([x[1:], x[:1]], 0)
    g = face(ext, f, s, [nxt(x) for x in ext], [nxt(x) for x in f], nxt(s))
    return [x[:rows] - jnp.concatenate([x[total - 1 :], x[: rows - 1]], 0) for x in g]


def ghost_rows(lo, hi, l):
    top = lax.broadcasted_iota(jnp.int32, (8, lo.shape[-1]), 0) < 4
    out = []
    for k in range(8):
        a = jnp.broadcast_to(hi[k, l : l + 1, :], top.shape)
        b = jnp.broadcast_to(lo[k, l : l + 1, :], top.shape)
        out.append(jnp.where(top, a, b))
    return out


def kernel(
    n, blocks, d_in, v_in, m_in, p_in, src_in, out_ref,
    d_ref, v_ref, m_ref, p_ref, src_ref, loads,
    state, part, lo0, hi0, ysend, ylo, yhi, psend, plo, phi,
    zsend, zlo, zhi, msend, mlo, mhi, full, full1, ghost, shell, glo, ghi, edges,
    xs, xr, ys, yr, ps, pr, zs, zr, ms, mr, fs, fr, hs, hr,
):
    layers, rows, lanes = d_ref.shape
    end = layers - 1
    corona, helio = blocks // 2, 3 * blocks // 8
    place, sec = lax.axis_index("blk"), lax.axis_index("sec")
    has_lo, has_hi = place > 0, place < blocks - 1
    coupled = (place == corona) | (place == corona + helio)
    source = (place + 1 == corona) | (place + 1 == corona + helio)

    def coeff(at):
        return 0.5 * jnp.where(
            at < corona,
            jnp.float32(0.05),
            jnp.where(at < corona + helio, jnp.float32(0.04), jnp.float32(0.055)),
        )

    c, c_lo, c_hi = coeff(place), coeff(place - 1), coeff(place + 1)
    others = [lax.rem(sec + k, n) for k in range(1, n)]
    north, south = others[0], others[-1]

    def remote(src, dst, s, r, **where):
        return pltpu.make_async_remote_copy(
            src_ref=src, dst_ref=dst, send_sem=s, recv_sem=r, device_id=where, device_id_type=MESH
        )

    def raw_layer(l, dst, s, r, **where):
        remote(d_in.at[pl.ds(l, 1)], dst.at[pl.ds(0, 1)], s, r, **where).start()
        remote(v_in.at[:, l], dst.at[pl.ds(1, 3)], s, r, **where).start()
        remote(m_in.at[:, l], dst.at[pl.ds(4, 3)], s, r, **where).start()
        remote(p_in.at[pl.ds(l, 1)], dst.at[pl.ds(7, 1)], s, r, **where).start()

    pairs = ((d_in, d_ref), (v_in, v_ref), (m_in, m_ref), (p_in, p_ref), (src_in, src_ref))
    reads = [pltpu.make_async_copy(a, b, loads.at[i]) for i, (a, b) in enumerate(pairs)]
    for read in reads:
        read.start()
    barrier = pltpu.get_barrier_semaphore()

    @pl.when(has_lo)
    def _():
        pl.semaphore_signal(barrier, inc=1, device_id={"blk": place - 1}, device_id_type=MESH)

    @pl.when(has_hi)
    def _():
        pl.semaphore_signal(barrier, inc=1, device_id={"blk": place + 1}, device_id_type=MESH)

    for o in others:
        pl.semaphore_signal(barrier, inc=1, device_id={"sec": o}, device_id_type=MESH)

    def raw(l):
        return (
            [d_ref[l]] + [v_ref[i, l] for i in range(3)] + [m_ref[i, l] for i in range(3)] + [p_ref[l]]
        )

    for read in reads:
        read.wait()
    for l in range(layers):
        for k, x in enumerate(raw(l)):
            ysend[0, k, l : l + 1, :] = x[:1]
            ysend[1, k, l : l + 1, :] = x[rows - 1 :]
    def x_flux(u):
        return flux(u, shared(u), 0)

    def keep(i, f, s):
        for k in range(8):
            if f[k] is not None:
                edges[i, k] = f[k]
        edges[i, 4] = s

    def kept(i):
        return [edges[i, k] if k != 4 else None for k in range(8)], edges[i, 4]

    def sweep(get, put):
        before = None
        for l in range(layers):
            u = get(l)
            sh = shared(u)
            fx, sx = flux(u, sh, 0)
            total = along_z(u, sh)
            if before is not None:
                pu, pf, ps_, ptotal = before
                g = face(pu, pf, ps_, u, fx, sx)
                put(l - 1, pu, [a + b for a, b in zip(ptotal, g)])
                total = [a - b for a, b in zip(total, g)]
            before = (u, fx, sx, total)
        put(end, before[0], before[3])

    def get0(l):
        u = conserve(raw(l))
        for k in range(8):
            state[k, l] = u[k]
        return u

    def put0(l, u, total):
        for k in range(8):
            part[k, l] = u[k] - c * total[k]

    sweep(get0, put0)
    pl.semaphore_wait(
        barrier, n - 1 + has_lo.astype(jnp.int32) + has_hi.astype(jnp.int32)
    )

    y_down = remote(ysend.at[0], yhi, ys.at[0], yr.at[0], sec=south)
    y_up = remote(ysend.at[1], ylo, ys.at[1], yr.at[1], sec=north)
    y_down.start()
    y_up.start()

    @pl.when(has_lo)
    def _():
        raw_layer(0, hi0, xs.at[0], xr.at[0], blk=place - 1)

    @pl.when(has_hi)
    def _():
        raw_layer(end, lo0, xs.at[1], xr.at[1], blk=place + 1)

    @pl.when(source)
    def _():
        for i, o in enumerate(others):
            raw_layer(end, full.at[sec], fs.at[i], fr.at[n - 2 - i], sec=o)
        for k, x in enumerate(raw(end)):
            full[sec, k] = x

    y_down.wait()
    y_up.wait()
    middle = list(range(1, end))

    def side1(l):
        u = [state[k, l] for k in range(8)]
        side = along_y(u, conserve(ghost_rows(ylo, yhi, l)))
        new = [part[k, l] - c * side[k] for k in range(8)]
        for k in range(8):
            part[k, l] = new[k]
        return new

    for l, i in ((0, 0), (end, 1)):
        for k, x in enumerate(side1(l)):
            psend[i, k] = x
    to_lo = remote(psend.at[0], phi, ps.at[0], pr.at[0], blk=place - 1)
    to_hi = remote(psend.at[1], plo, ps.at[1], pr.at[1], blk=place + 1)

    @pl.when(has_lo)
    def _():
        to_lo.start()

    @pl.when(has_hi)
    def _():
        to_hi.start()

    for i, l in enumerate(middle):
        for k, x in enumerate(side1(l)):
            msend[0, k, i : i + 1, :] = x[:1]
            msend[1, k, i : i + 1, :] = x[rows - 1 :]
    m_down = remote(msend.at[0], mhi, ms.at[0], mr.at[0], sec=south)
    m_up = remote(msend.at[1], mlo, ms.at[1], mr.at[1], sec=north)
    m_down.start()
    m_up.start()

    before = None
    for l in middle:
        u = [part[k, l] for k in range(8)]
        sh = shared(u)
        fx, sx = flux(u, sh, 0)
        total = along_z(u, sh)
        if l == middle[0]:
            keep(0, fx, sx)
        if l == middle[-1]:
            keep(1, fx, sx)
        if before is not None:
            pu, pf, ps_, ptotal = before
            g = face(pu, pf, ps_, u, fx, sx)
            for k in range(8):
                state[k, l - 1] = ptotal[k] + g[k]
            total = [a - b for a, b in zip(total, g)]
        before = (u, fx, sx, total)
    for k in range(8):
        state[k, middle[-1]] = before[3][k]
    m_down.wait()
    m_up.wait()
    for i, l in enumerate(middle):
        side = along_y([part[k, l] for k in range(8)], ghost_rows(mlo, mhi, i))
        for k in range(8):
            state[k, l] = state[k, l] + side[k]

    raw_lo = remote(hi0, lo0, xs.at[1], xr.at[1], blk=place + 1)
    raw_hi = remote(lo0, hi0, xs.at[0], xr.at[0], blk=place - 1)

    @pl.when(has_lo)
    def _():
        raw_lo.wait_recv()

    @pl.when(jnp.logical_not(has_lo))
    def _():
        for k, x in enumerate(raw(0)):
            lo0[k] = x

    @pl.when(coupled)
    def _():
        for i, o in enumerate(others):
            remote(lo0, full.at[sec], fs.at[i], fr.at[n - 2 - i], sec=o).start()
        for k in range(8):
            full[sec, k] = lo0[k]

    @pl.when(has_hi)
    def _():
        raw_hi.wait_recv()

    @pl.when(jnp.logical_not(has_hi))
    def _():
        for k, x in enumerate(raw(end)):
            hi0[k] = x

    second = place + 1 >= corona + helio
    index = jnp.where(second, src_ref[1], src_ref[0])
    index_y, index_z = lax.div(index, lanes), lax.rem(index, lanes)

    def gather(ref, s, acc):
        def body(t, acc):
            here = index_y == s * rows + t
            new = []
            for k in range(8):
                line = jnp.broadcast_to(ref[s, k, pl.ds(t, 1), :], index.shape)
                got = jnp.take_along_axis(line, index_z, axis=1, mode="promise_in_bounds")
                new.append(jnp.where(here, got, acc[k]))
            return tuple(new)

        return lax.fori_loop(0, rows, body, acc, unroll=8)

    def gather_all(ref, arrived):
        acc = gather(ref, sec, (jnp.zeros(index.shape, jnp.float32),) * 8)
        for i in range(n - 1):
            arrived(i).wait_recv()
            acc = gather(ref, others[i], acc)
        return acc

    def load(ref):
        return [ref[k] for k in range(8)]

    def own(l):
        return [state[k, l] for k in range(8)]

    arrived0 = lambda i: remote(lo0, full.at[others[i]], fs.at[i], fr.at[i], sec=others[i])
    arrived1 = lambda i: remote(glo, full1.at[others[i]], hs.at[i], hr.at[i], sec=others[i])

    u_lo, u_hi = conserve(load(lo0)), conserve(load(hi0))
    u0, ue = own(0), own(end)
    f0, s0 = x_flux(u0)
    fe, se = x_flux(ue)
    fh, sh_ = x_flux(u_hi)
    g_out = face(ue, fe, se, u_hi, fh, sh_)
    g_true = face(u_lo, *x_flux(u_lo), u0, f0, s0)
    for k in range(8):
        new = part[k, end] - c * g_out[k]
        part[k, end] = new
        zsend[0, k, 1:2, :] = new[:1]
        zsend[1, k, 1:2, :] = new[rows - 1 :]
        shell[k] = g_true[k]

    def get1(l):
        return [part[k, l] for k in range(8)]

    ve = get1(end)
    he = shared(ve)
    pe, qe = flux(ve, he, 0)
    above = face(get1(end - 1), *kept(1), ve, pe, qe)
    ze = along_z(ve, he)
    for k in range(8):
        state[k, end] = ze[k] - above[k]
        state[k, end - 1] = state[k, end - 1] + above[k]

    @pl.when(coupled)
    def _():
        inner = conserve(gather_all(full, arrived0))
        for k, x in enumerate(face(inner, *x_flux(inner), u0, f0, s0)):
            shell[k] = x

    for k in range(8):
        part[k, 0] = part[k, 0] + c * shell[k]
    for k in range(8):
        zsend[0, k, 0:1, :] = part[k, 0, :1, :]
        zsend[1, k, 0:1, :] = part[k, 0, rows - 1 :, :]
    z_down = remote(zsend.at[0], zhi, zs.at[0], zr.at[0], sec=south)
    z_up = remote(zsend.at[1], zlo, zs.at[1], zr.at[1], sec=north)
    z_down.start()
    z_up.start()

    @pl.when(coupled)
    def _():
        to_hi.wait_recv()
        for k in range(8):
            new = plo[k] - c_lo * g_true[k]
            glo[k] = new
            full1[sec, k] = new
        for i, o in enumerate(others):
            remote(glo, full1.at[sec], hs.at[i], hr.at[n - 2 - i], sec=o).start()

    for k in range(8):
        ghi[k] = g_out[k]

    @pl.when(source)
    def _():
        low = conserve(gather_all(full, arrived0))
        for k, x in enumerate(face(low, *x_flux(low), u_hi, fh, sh_)):
            ghi[k] = x

    v0 = get1(0)
    h0 = shared(v0)
    p0, q0 = flux(v0, h0, 0)
    below = face(v0, p0, q0, get1(1), *kept(0))
    z0 = along_z(v0, h0)
    for k in range(8):
        state[k, 0] = z0[k] + below[k]
        state[k, 1] = state[k, 1] - below[k]
    for l in middle:
        for k in range(8):
            out_ref[k, l] = part[k, l] - c * state[k, l]
    z_down.wait()
    z_up.wait()
    for i, l in enumerate((0, end)):
        side = along_y(get1(l), ghost_rows(zlo, zhi, i))
        for k in range(8):
            state[k, l] = state[k, l] + side[k]

    @pl.when(has_hi)
    def _():
        to_lo.wait_recv()
        for k in range(8):
            ghi[k] = phi[k] + c_hi * ghi[k]

    @pl.when(jnp.logical_not(has_hi))
    def _():
        for k in range(8):
            ghi[k] = part[k, end]

    @pl.when(jnp.logical_not(has_lo))
    def _():
        for k in range(8):
            ghost[k] = part[k, 0]

    @pl.when(has_lo & jnp.logical_not(coupled))
    def _():
        to_hi.wait_recv()
        for k in range(8):
            ghost[k] = plo[k] - c_lo * shell[k]

    @pl.when(coupled)
    def _():
        for k, x in enumerate(gather_all(full1, arrived1)):
            ghost[k] = x

    low, high = load(ghost), load(ghi)
    g_low = face(low, *x_flux(low), v0, p0, q0)
    g_high = face(ve, pe, qe, high, *x_flux(high))
    for k in range(8):
        out_ref[k, 0] = v0[k] - c * (state[k, 0] - g_low[k])
        out_ref[k, end] = ve[k] - c * (state[k, end] + g_high[k])

    @pl.when(has_lo)
    def _():
        raw_hi.wait_send()
        to_lo.wait_send()

    @pl.when(has_hi)
    def _():
        raw_lo.wait_send()
        to_hi.wait_send()

    @pl.when(coupled | source)
    def _():
        for i, o in enumerate(others):
            remote(lo0, full.at[sec], fs.at[i], fr.at[i], sec=o).wait_send()

    @pl.when(coupled)
    def _():
        for i, o in enumerate(others):
            remote(glo, full1.at[sec], hs.at[i], hr.at[i], sec=o).wait_send()


def local(density, velocity, magnetic, pressure, shell_source):
    n, blocks = lax.axis_size("sec"), lax.axis_size("blk")
    layers, rows, lanes = density.shape
    vm = lambda *shape: pltpu.VMEM(shape, jnp.float32)
    dma = lambda k: pltpu.SemaphoreType.DMA((k,))
    plane = (8, rows, lanes)
    edge, pair, mids = [(8, k, lanes) for k in (layers, 2, layers - 2)]
    vmem = pl.BlockSpec(memory_space=pltpu.VMEM)
    hold = lambda x: pltpu.with_memory_space_constraint(x, pltpu.HBM)
    return pl.pallas_call(
        functools.partial(kernel, n, blocks),
        out_shape=jax.ShapeDtypeStruct((8,) + density.shape, jnp.float32),
        in_specs=[pl.BlockSpec(memory_space=pltpu.HBM)] * 5,
        out_specs=vmem,
        scratch_shapes=[
            vm(layers, rows, lanes), vm(3, layers, rows, lanes), vm(3, layers, rows, lanes),
            vm(layers, rows, lanes), pltpu.VMEM(shell_source.shape, jnp.int32), dma(5),
            vm(8, layers, rows, lanes), vm(8, layers, rows, lanes),
            vm(*plane), vm(*plane), vm(2, *edge), vm(*edge), vm(*edge),
            vm(2, *plane), vm(*plane), vm(*plane),
            vm(2, *pair), vm(*pair), vm(*pair), vm(2, *mids), vm(*mids), vm(*mids),
            vm(n, *plane), vm(n, *plane), vm(*plane), vm(*plane), vm(*plane), vm(*plane), vm(2, *plane),
            dma(2), dma(2), dma(2), dma(2), dma(2), dma(2), dma(2), dma(2), dma(2), dma(2),
            dma(n - 1), dma(n - 1), dma(n - 1), dma(n - 1),
        ],
        compiler_params=pltpu.CompilerParams(vmem_limit_bytes=8 * 2**20, collective_id=0, has_side_effects=True),
    )(*map(hold, (density, velocity, magnetic, pressure, shell_source)))


def solution(mesh):
    return jax.shard_map(
        local,
        mesh=mesh,
        in_specs=(
            P("blk", "sec", None),
            P(None, "blk", "sec", None),
            P(None, "blk", "sec", None),
            P("blk", "sec", None),
            P(None, "sec", None),
        ),
        out_specs=P(None, "blk", "sec", None),
        check_vma=False,
    )
```
